512 devices in a mesh: row: 32 (over z, y_lo), col: 16 (over x, y_hi, core).
Axes of the slice: x: 4, y: 4 (y_hi: 2, y_lo: 2; y = y_hi * 2 + y_lo), z: 16, core: 2. Of those that a mesh axis runs over, the one named last changes fastest.
Arguments:
- pair_in: bfloat16 [384, 384, 128], P('row', 'col'), may hold values from -6 to 6
- cotangent: bfloat16 [384, 384, 128], P('row', 'col'), may hold values from -6 to 6
- in_gain: float32 [128], replicated, may hold values from 0.25 to 1.75
- in_bias: float32 [128], replicated, may hold values from -3 to 3
- in_weights: bfloat16 [128, 640], replicated, may hold values from -0.5 to 0.5
- out_gain: float32 [128], replicated, may hold values from 0.25 to 1.75
- out_bias: float32 [128], replicated, may hold values from -3 to 3
- out_weights: bfloat16 [128, 128], replicated, may hold values from -0.5 to 0.5
Outputs:
- pair_out: bfloat16 [384, 384, 128], P('row', 'col')
- grad_pair: bfloat16 [384, 384, 128], P('row', 'col')
- grad_in_weights: float32 [128, 640], replicated
- grad_out_weights: float32 [128, 128], replicated
- grad_norms: float32 [4, 128], replicated
The draws below stay inside these ranges and needn't reach their ends.
All inputs are finite; a program needn't handle non-finite values.
Results may differ from the reference program's by a relative error of at most 0.015.
Values may be sent and summed in bfloat16 or wider, within the bound.
No kernel may reach another device: no remote copies, remote signals or barrier semaphores. Data moves between devices by JAX's collectives and lax.ppermute only.
A program may use at most 64 MiB of HBM per device.

```python
import jax
import jax.numpy as jnp
from jax import lax

C = 128
R_DEV = 12
N_RES = 384
C_DEV = 24
N_ROW = 32
N_COL = 16


def levels(key, shape, pieces, smallest, top_value):
    def one(axis_at, shards_of):
        steps = jax.random.uniform(jax.random.fold_in(jax.random.fold_in(key, 6), axis_at), (shards_of,), jnp.float32, smallest / len(pieces), top_value / len(pieces))
        return jnp.repeat(jnp.exp(steps), shape[axis_at] // shards_of).reshape((-1,) + (1,) * (len(shape) - axis_at - 1))

    loudness = one(*pieces[0])
    for cut in pieces[1:]:
        loudness = loudness * one(*cut)
    return loudness


def scatter_about(own_key, extent, spread, reach, cuts=(), kind=jnp.bfloat16):
    loudness = levels(own_key, extent, cuts, -0.22, 0.18) if cuts else 1.0
    entries = jax.random.normal(own_key, extent, jnp.float32) * spread * loudness
    return jnp.minimum(jnp.maximum(entries, -reach), reach).astype(kind)


def setup_inputs(seed: int = 0) -> dict:
    key_of = jax.random.split(jax.random.key(seed), 9)
    pair_in = scatter_about(key_of[0], (N_RES, N_RES, C), 1.0, 6.0, ((0, 32), (1, 16)))
    cotangent = scatter_about(key_of[1], (N_RES, N_RES, C), 1.0, 6.0, ((0, 32), (1, 16)))
    in_gain = jnp.clip(1.0 + 0.15 * jax.random.normal(key_of[2], (C,), jnp.float32), 0.25, 1.75)
    in_bias = scatter_about(key_of[3], (C,), 0.5, 3.0, (), jnp.float32)
    in_weights = scatter_about(key_of[4], (C, 5 * C), C ** -0.5, 0.5)
    out_gain = jnp.clip(1.0 + 0.15 * jax.random.normal(key_of[5], (C,), jnp.float32), 0.25, 1.75)
    out_bias = scatter_about(key_of[6], (C,), 0.5, 3.0, (), jnp.float32)
    out_weights = scatter_about(key_of[7], (C, C), C ** -0.5, 0.5)
    return dict(pair_in=pair_in, cotangent=cotangent, in_gain=in_gain, in_bias=in_bias, in_weights=in_weights, out_gain=out_gain, out_bias=out_bias, out_weights=out_weights)


def layer_stats(values):
    average = lax.optimization_barrier(jnp.mean(values, axis=-1, keepdims=True))
    centred = values - average
    inv_std = lax.rsqrt(lax.optimization_barrier(jnp.mean(centred * centred, axis=-1, keepdims=True)) + 1e-05)
    return (centred * inv_std, inv_std)

def layer_back(upstream, normal_hat, inv_std, scaling):
    scaled = upstream * scaling
    bracket = scaled - lax.optimization_barrier(jnp.mean(scaled, axis=-1, keepdims=True)) - normal_hat * lax.optimization_barrier(jnp.mean(scaled * normal_hat, axis=-1, keepdims=True))
    return inv_std * bracket

def reference(pair_in, cotangent, in_gain, in_bias, in_weights, out_gain, out_bias, out_weights):
    in_hat, in_rstd = layer_stats(pair_in.astype(jnp.float32))
    in_norm = (in_hat * in_gain + in_bias).astype(jnp.bfloat16)
    projected = jnp.einsum('ijc,cd->ijd', in_norm.astype(jnp.float32), in_weights.astype(jnp.float32))
    lin_left = projected[:, :, :C]
    left_sig = jax.nn.sigmoid(projected[:, :, C:2 * C])
    lin_right = projected[:, :, 2 * C:3 * C]
    right_sig = jax.nn.sigmoid(projected[:, :, 3 * C:4 * C])
    gate_act = jax.nn.sigmoid(projected[:, :, 4 * C:])
    left_act = (left_sig * lin_left).astype(jnp.bfloat16)
    right_act = (right_sig * lin_right).astype(jnp.bfloat16)
    product = jnp.einsum('ikc,jkc->ijc', left_act.astype(jnp.float32), right_act.astype(jnp.float32))
    out_hat, out_rstd = layer_stats(product)
    out_norm = (out_hat * out_gain + out_bias).astype(jnp.bfloat16)
    out_lin = jnp.einsum('ijc,cd->ijd', out_norm.astype(jnp.float32), out_weights.astype(jnp.float32))
    pair_out = (gate_act * out_lin).astype(jnp.bfloat16)
    upstream = cotangent.astype(jnp.float32)
    d_lin = (upstream * gate_act).astype(jnp.bfloat16)
    d_gate = upstream * out_lin
    d_outnorm = jnp.einsum('ijd,cd->ijc', d_lin.astype(jnp.float32), out_weights.astype(jnp.float32))
    d_product = layer_back(d_outnorm, out_hat, out_rstd, out_gain).astype(jnp.bfloat16)

    def column_term(column, running):
        start = (column * C_DEV).astype(jnp.int32)
        d_piece = lax.dynamic_slice_in_dim(d_product, start, C_DEV, 1).astype(jnp.float32)
        r_piece = lax.dynamic_slice_in_dim(right_act, start, C_DEV, 0).astype(jnp.float32)
        term = jnp.einsum('ijc,jkc->ikc', d_piece, r_piece)
        term = lax.optimization_barrier(term.astype(jnp.bfloat16)).astype(jnp.float32)
        return running + term

    def row_term(rowblock, running):
        start = (rowblock * R_DEV).astype(jnp.int32)
        d_piece = lax.dynamic_slice_in_dim(d_product, start, R_DEV, 0).astype(jnp.float32)
        l_piece = lax.dynamic_slice_in_dim(left_act, start, R_DEV, 0).astype(jnp.float32)
        term = jnp.einsum('ijc,ikc->jkc', d_piece, l_piece)
        term = lax.optimization_barrier(term.astype(jnp.bfloat16)).astype(jnp.float32)
        return running + term
    zeros_pair = jnp.zeros((N_RES, N_RES, C), jnp.float32)
    d_left = lax.fori_loop(0, N_COL, column_term, zeros_pair)
    d_right = lax.fori_loop(0, N_ROW, row_term, zeros_pair)
    d_proj = jnp.concatenate([d_left * left_sig, d_left * lin_left * left_sig * (1.0 - left_sig), d_right * right_sig, d_right * lin_right * right_sig * (1.0 - right_sig), d_gate * gate_act * (1.0 - gate_act)], axis=-1).astype(jnp.bfloat16)
    d_innorm = jnp.einsum('ijd,cd->ijc', d_proj.astype(jnp.float32), in_weights.astype(jnp.float32))
    grad_pair = layer_back(d_innorm, in_hat, in_rstd, in_gain).astype(jnp.bfloat16)
    per_residue = 1.0 / N_RES
    grad_in_weights = jnp.einsum('ijc,ijd->cd', in_norm.astype(jnp.float32), d_proj.astype(jnp.float32)) * per_residue
    grad_out_weights = jnp.einsum('ijc,ijd->cd', out_norm.astype(jnp.float32), d_lin.astype(jnp.float32)) * per_residue
    grad_norms = jnp.stack([lax.optimization_barrier(jnp.sum(d_innorm * in_hat, axis=(0, 1))), lax.optimization_barrier(jnp.sum(d_innorm, axis=(0, 1))), lax.optimization_barrier(jnp.sum(d_outnorm * out_hat, axis=(0, 1))), lax.optimization_barrier(jnp.sum(d_outnorm, axis=(0, 1)))]) * per_residue
    return (pair_out, grad_pair, grad_in_weights, grad_out_weights, grad_norms)
```

```python
import jax
import jax.numpy as jnp
from jax import lax
from jax.sharding import Mesh, PartitionSpec as P

GROUP = ("rr", "col")
BF = jnp.bfloat16
F32 = jnp.float32


def dot(a, b, da, db):
    return lax.dot_general(a, b, (((da,), (db,)), ((), ())), preferred_element_type=F32)


def stats(values, axis):
    average = jnp.mean(values, axis=axis, keepdims=True)
    centred = values - average
    inv_std = lax.rsqrt(jnp.mean(centred * centred, axis=axis, keepdims=True) + 1e-05)
    return centred * inv_std, inv_std


def back(upstream, hat, inv_std, scaling, axis):
    scaled = upstream * scaling
    return inv_std * (
        scaled
        - jnp.mean(scaled, axis=axis, keepdims=True)
        - hat * jnp.mean(scaled * hat, axis=axis, keepdims=True)
    )


def exchange(x):
    return lax.all_to_all(x, GROUP, split_axis=0, concat_axis=0, tiled=True)


def local(pair_in, cotangent, in_gain, in_bias, in_weights, out_gain, out_bias, out_weights):
    ni, nk, c = pair_in.shape
    rr, cols, rq = lax.axis_size("rr"), lax.axis_size("col"), lax.axis_size("rq")
    pairs = ni * nk
    rows, all_k = rr * ni, cols * nk

    def to_matrix(x):
        x = x.reshape(rr, cols, -1, ni, nk).transpose(2, 0, 3, 1, 4)
        return x.reshape(-1, rows, all_k)

    def from_matrix(x):
        x = x.reshape(-1, rr, ni, cols, nk).transpose(1, 3, 0, 2, 4)
        return x.reshape(c, -1)

    in_hat, in_rstd = stats(pair_in.reshape(pairs, c).astype(F32), 1)
    in_norm = (in_hat * in_gain + in_bias).astype(BF)
    w_gate = in_weights[:, 4 * c :]
    proj = dot(in_weights[:, : 4 * c], in_norm, 0, 1)
    gate = jax.nn.sigmoid(dot(in_norm, w_gate, 1, 0))
    lin_left, lin_right = proj[:c], proj[2 * c : 3 * c]
    left_sig = jax.nn.sigmoid(proj[c : 2 * c])
    right_sig = jax.nn.sigmoid(proj[3 * c :])
    left = (left_sig * lin_left).astype(BF)
    right = (right_sig * lin_right).astype(BF)

    got = exchange(jnp.concatenate([left, right], axis=1))
    mats = to_matrix(got)
    gathered = lax.all_gather(mats, "rq")
    left_all = gathered[:, 0].reshape(rq * rows, all_k)
    right_all = gathered[:, 1].reshape(rq * rows, all_k)
    product = dot(mats[0], right_all, 1, 1)
    prod = exchange(from_matrix(product))

    out_hat, out_rstd = stats(prod, 0)
    gain_col = out_gain[:, None]
    out_norm = (out_hat * gain_col + out_bias[:, None]).astype(BF)
    out_lin = dot(out_norm, out_weights, 0, 0)
    pair_out = (gate * out_lin).astype(BF)
    upstream = cotangent.reshape(pairs, c).astype(F32)
    d_lin = (upstream * gate).astype(BF)
    d_gate = upstream * out_lin
    d_outnorm = dot(out_weights, d_lin, 1, 1)
    d_product = back(d_outnorm, out_hat, out_rstd, gain_col, 0).astype(BF)

    d_mat = to_matrix(exchange(d_product))[0]
    d_all = lax.all_gather(d_mat, "rq").reshape(rq * rows, all_k)
    d_left_m = dot(d_mat, right_all, 1, 0).astype(BF)
    d_right_m = dot(d_all, left_all, 0, 0).astype(BF)
    d_right_m = lax.dynamic_slice_in_dim(d_right_m, lax.axis_index("rq") * rows, rows, 0)
    d_both = exchange(from_matrix(jnp.stack([d_left_m, d_right_m]))).astype(F32)
    d_left, d_right = d_both[:, :pairs], d_both[:, pairs:]

    d_proj = [
        (d_left * left_sig).astype(BF),
        (d_left * lin_left * left_sig * (1.0 - left_sig)).astype(BF),
        (d_right * right_sig).astype(BF),
        (d_right * lin_right * right_sig * (1.0 - right_sig)).astype(BF),
    ]
    d_five = (d_gate * gate * (1.0 - gate)).astype(BF)
    d_innorm = dot(jnp.concatenate(d_proj), in_weights[:, : 4 * c], 0, 1) + dot(d_five, w_gate, 1, 1)
    grad_pair = back(d_innorm, in_hat, in_rstd, in_gain, 1).astype(BF)

    norms = jnp.stack(
        [
            jnp.sum(d_innorm * in_hat, axis=0),
            jnp.sum(d_innorm, axis=0),
            jnp.sum(d_outnorm * out_hat, axis=1),
            jnp.sum(d_outnorm, axis=1),
        ]
    )
    blocks = [dot(in_norm, part, 0, 1) for part in d_proj]
    blocks += [dot(in_norm, d_five, 0, 0), dot(out_norm, d_lin, 1, 0), norms]
    used = 6 * c + 4
    slots = 8 * c
    stacked = jnp.concatenate(blocks + [jnp.zeros((slots - used, c), F32)])
    mine = jnp.sum(exchange(stacked.reshape(c, 8, c)), axis=0)
    quarter = lax.all_gather(mine, "rq")
    total = (quarter[0] + quarter[1]) + (quarter[2] + quarter[3])
    total = total * (1.0 / all_k)
    summed = exchange(jnp.broadcast_to(total[None], (c, 8, c))).reshape(slots, c)
    grad_in = jnp.concatenate([summed[b * c : (b + 1) * c] for b in range(5)], axis=1)
    return (
        pair_out.reshape(ni, nk, c),
        grad_pair.reshape(ni, nk, c),
        grad_in,
        summed[5 * c : 6 * c],
        summed[6 * c : used],
    )


def solution(mesh):
    grid = mesh.devices.reshape(4, mesh.devices.shape[0] // 4, mesh.devices.shape[1])
    split = Mesh(grid, ("rq", "rr", "col"))
    pair = P(("rq", "rr"), "col", None)
    return jax.shard_map(
        local,
        mesh=split,
        in_specs=(pair, pair, P(), P(), P(), P(), P(), P()),
        out_specs=(pair, pair, P(), P(), P()),
        check_vma=False,
    )
```

```python
import jax
import jax.numpy as jnp
from jax import lax
from jax.sharding import Mesh, PartitionSpec as P

GROUP = ("row", "xh", "yh")
QUAD = ("xl", "core")
BF = jnp.bfloat16
F32 = jnp.float32


def dot(a, b, da, db):
    return lax.dot_general(a, b, (((da,), (db,)), ((), ())), preferred_element_type=F32)


def stats(values, axis):
    average = jnp.mean(values, axis=axis, keepdims=True)
    centred = values - average
    inv_std = lax.rsqrt(jnp.mean(centred * centred, axis=axis, keepdims=True) + 1e-05)
    return centred * inv_std, inv_std


def back(upstream, hat, inv_std, scaling, axis):
    scaled = upstream * scaling
    return inv_std * (
        scaled
        - jnp.mean(scaled, axis=axis, keepdims=True)
        - hat * jnp.mean(scaled * hat, axis=axis, keepdims=True)
    )


def exchange(x):
    return lax.all_to_all(x, GROUP, split_axis=0, concat_axis=0, tiled=True)


def local(pair_in, cotangent, in_gain, in_bias, in_weights, out_gain, out_bias, out_weights):
    ni, nk, c = pair_in.shape
    nrow, quads = lax.axis_size("row"), 4
    pairs = ni * nk
    rows, part = nrow * ni, quads * nk
    quad = lax.axis_index(QUAD)

    def to_matrix(x):
        return x.reshape(nrow, quads, ni, nk).transpose(0, 2, 1, 3).reshape(rows, part)

    def from_matrix(x):
        return x.reshape(nrow, ni, quads, nk).transpose(0, 2, 1, 3).reshape(c, pairs)

    def to_blocks(x):
        x = x.reshape(2, 2, 2, 2, nk // ni, quads, ni, nk).transpose(1, 3, 0, 2, 4, 6, 5, 7)
        return x.reshape(quads, part, part)

    def from_blocks(x):
        x = x.reshape(2, 2, 2, 2, nk // ni, ni, quads, nk).transpose(2, 0, 3, 1, 4, 6, 5, 7)
        return x.reshape(c, pairs)

    in_hat, in_rstd = stats(pair_in.reshape(pairs, c).astype(F32), 1)
    in_norm = (in_hat * in_gain + in_bias).astype(BF)
    w_gate = in_weights[:, 4 * c :]
    proj = dot(in_weights[:, : 4 * c], in_norm, 0, 1)
    gate = jax.nn.sigmoid(dot(in_norm, w_gate, 1, 0))
    lin_left, lin_right = proj[:c], proj[2 * c : 3 * c]
    left_sig = jax.nn.sigmoid(proj[c : 2 * c])
    right_sig = jax.nn.sigmoid(proj[3 * c :])
    left = (left_sig * lin_left).astype(BF)
    right = (right_sig * lin_right).astype(BF)

    got = exchange(jnp.concatenate([left, right], axis=1))
    left_own = to_matrix(got[:, :pairs])
    right_own = to_blocks(got[:, pairs:])
    gathered = lax.all_gather(jnp.stack([left_own, right_own.reshape(rows, part)]), QUAD)
    product = jnp.zeros((rows, part), F32)
    for q in range(quads):
        picked = lax.dynamic_slice_in_dim(gathered[q, 1], quad * part, part, 0)
        product = product + dot(gathered[q, 0], picked, 1, 1)
    prod = exchange(from_matrix(product))

    out_hat, out_rstd = stats(prod, 0)
    gain_col = out_gain[:, None]
    out_norm = (out_hat * gain_col + out_bias[:, None]).astype(BF)
    out_lin = dot(out_norm, out_weights, 0, 0)
    pair_out = (gate * out_lin).astype(BF)
    upstream = cotangent.reshape(pairs, c).astype(F32)
    d_lin = (upstream * gate).astype(BF)
    d_gate = upstream * out_lin
    d_outnorm = dot(out_weights, d_lin, 1, 1)
    d_product = back(d_outnorm, out_hat, out_rstd, gain_col, 0).astype(BF)

    d_all = lax.all_gather(to_matrix(exchange(d_product)), QUAD)
    d_left_m = jnp.zeros((rows, part), F32)
    d_right_m = []
    for q in range(quads):
        d_left_m = d_left_m + dot(d_all[q], right_own[q], 1, 0)
        d_right_m.append(dot(d_all[q], left_own, 0, 0).astype(BF))
    d_left_s = from_matrix(d_left_m.astype(BF))
    d_right_s = from_blocks(jnp.concatenate(d_right_m))
    d_both = exchange(jnp.concatenate([d_left_s, d_right_s], axis=1)).astype(F32)
    d_left, d_right = d_both[:, :pairs], d_both[:, pairs:]

    d_proj = [
        (d_left * left_sig).astype(BF),
        (d_left * lin_left * left_sig * (1.0 - left_sig)).astype(BF),
        (d_right * right_sig).astype(BF),
        (d_right * lin_right * right_sig * (1.0 - right_sig)).astype(BF),
    ]
    d_five = (d_gate * gate * (1.0 - gate)).astype(BF)
    d_innorm = dot(jnp.concatenate(d_proj), in_weights[:, : 4 * c], 0, 1) + dot(d_five, w_gate, 1, 1)
    grad_pair = back(d_innorm, in_hat, in_rstd, in_gain, 1).astype(BF)

    norms = jnp.stack(
        [
            jnp.sum(d_innorm * in_hat, axis=0),
            jnp.sum(d_innorm, axis=0),
            jnp.sum(d_outnorm * out_hat, axis=1),
            jnp.sum(d_outnorm, axis=1),
        ]
    )
    blocks = [dot(in_norm, d, 0, 1) for d in d_proj]
    blocks += [dot(in_norm, d_five, 0, 0), dot(out_norm, d_lin, 1, 0), norms]
    used, share, slots = 6 * c + 4, 200, 2
    stacked = jnp.concatenate(blocks + [jnp.zeros((quads * share - used, c), F32)])
    ours = lax.all_to_all(
        stacked.reshape(quads, share, c), QUAD, split_axis=0, concat_axis=0, tiled=True
    )
    ours = jnp.pad(jnp.sum(ours, axis=0), ((0, slots * c - share), (0, 0)))
    mine = jnp.sum(exchange(ours.reshape(c, slots, c)), axis=0) * (1.0 / rows)
    summed = exchange(jnp.broadcast_to(mine[None], (c, slots, c))).reshape(slots * c, c)
    summed = lax.all_gather(summed[:share], QUAD).reshape(quads * share, c)
    grad_in = jnp.concatenate([summed[b * c : (b + 1) * c] for b in range(5)], axis=1)
    return (
        pair_out.reshape(ni, nk, c),
        grad_pair.reshape(ni, nk, c),
        grad_in,
        summed[5 * c : 6 * c],
        summed[6 * c : used],
    )


def solution(mesh):
    grid = mesh.devices.reshape(mesh.devices.shape[0], 2, 2, 2, 2)
    split = Mesh(grid, ("row", "xh", "xl", "yh", "core"))
    pair = P("row", ("xh", "xl", "yh", "core"), None)
    return jax.shard_map(
        local,
        mesh=split,
        in_specs=(pair, pair, P(), P(), P(), P(), P(), P()),
        out_specs=(pair, pair, P(), P(), P()),
        check_vma=False,
    )
```

```python
import jax
import jax.numpy as jnp
from jax import lax
from jax.sharding import Mesh, PartitionSpec as P

CUBE = ("zr", "yl", "xh", "xl", "yh", "core")
MID = ("zr", "yl", "xh", "yh")
QUAD = ("xl", "core")
BF = jnp.bfloat16
F32 = jnp.float32


def dot(a, b, da, db):
    return lax.dot_general(a, b, (((da,), (db,)), ((), ())), preferred_element_type=F32)


def stats(values, axis):
    average = jnp.mean(values, axis=axis, keepdims=True)
    centred = values - average
    inv_std = lax.rsqrt(jnp.mean(centred * centred, axis=axis, keepdims=True) + 1e-05)
    return centred * inv_std, inv_std


def back(upstream, hat, inv_std, scaling, axis):
    scaled = upstream * scaling
    return inv_std * (
        scaled
        - jnp.mean(scaled, axis=axis, keepdims=True)
        - hat * jnp.mean(scaled * hat, axis=axis, keepdims=True)
    )


def exchange(x, axes=CUBE):
    return lax.all_to_all(x, axes, split_axis=0, concat_axis=0, tiled=True)


def local(pair_in, cotangent, in_gain, in_bias, in_weights, out_gain, out_bias, out_weights):
    ni, nk, c = pair_in.shape
    rr, cols, quarters = 8, 16, 4
    pairs = ni * nk
    rows, all_k = rr * ni, cols * nk

    def to_matrix(x):
        x = x.reshape(rr, cols, ni, nk).transpose(0, 2, 1, 3)
        return x.reshape(rows, all_k)

    def from_matrix(x):
        x = x.reshape(rr, ni, cols, nk).transpose(0, 2, 1, 3)
        return x.reshape(c, pairs)

    in_hat, in_rstd = stats(pair_in.reshape(pairs, c).astype(F32), 1)
    in_norm = (in_hat * in_gain + in_bias).astype(BF)
    w_gate = in_weights[:, 4 * c :]
    proj = dot(in_weights[:, : 4 * c], in_norm, 0, 1)
    gate = jax.nn.sigmoid(dot(in_norm, w_gate, 1, 0))
    lin_left, lin_right = proj[:c], proj[2 * c : 3 * c]
    left_sig = jax.nn.sigmoid(proj[c : 2 * c])
    right_sig = jax.nn.sigmoid(proj[3 * c :])
    left = (left_sig * lin_left).astype(BF)
    right = (right_sig * lin_right).astype(BF)

    got = exchange(jnp.concatenate([left, right], axis=1))
    left_own = to_matrix(got[:, :pairs])
    right_all = lax.all_gather(to_matrix(got[:, pairs:]), "zq").reshape(all_k, all_k)
    product = dot(left_own, right_all, 1, 1)
    prod = exchange(from_matrix(product))

    out_hat, out_rstd = stats(prod, 0)
    gain_col = out_gain[:, None]
    out_norm = (out_hat * gain_col + out_bias[:, None]).astype(BF)
    out_lin = dot(out_norm, out_weights, 0, 0)
    pair_out = (gate * out_lin).astype(BF)
    upstream = cotangent.reshape(pairs, c).astype(F32)
    d_lin = (upstream * gate).astype(BF)
    d_gate = upstream * out_lin
    d_outnorm = dot(out_weights, d_lin, 1, 1)
    d_product = back(d_outnorm, out_hat, out_rstd, gain_col, 0).astype(BF)

    d_mat = to_matrix(exchange(d_product))
    d_left_m = dot(d_mat, right_all, 1, 0).astype(BF)
    terms = dot(d_mat, left_own, 0, 0).astype(BF)
    terms = exchange(terms.reshape(quarters, rows, all_k), ("zq",))
    d_right_m = jnp.sum(terms.astype(F32), axis=0).astype(BF)
    d_both = exchange(jnp.concatenate([from_matrix(d_left_m), from_matrix(d_right_m)], axis=1))
    d_both = d_both.astype(F32)
    d_left, d_right = d_both[:, :pairs], d_both[:, pairs:]

    d_proj = [
        (d_left * left_sig).astype(BF),
        (d_left * lin_left * left_sig * (1.0 - left_sig)).astype(BF),
        (d_right * right_sig).astype(BF),
        (d_right * lin_right * right_sig * (1.0 - right_sig)).astype(BF),
    ]
    d_five = (d_gate * gate * (1.0 - gate)).astype(BF)
    d_innorm = dot(jnp.concatenate(d_proj), in_weights[:, : 4 * c], 0, 1) + dot(d_five, w_gate, 1, 1)
    grad_pair = back(d_innorm, in_hat, in_rstd, in_gain, 1).astype(BF)

    norms = jnp.stack(
        [
            jnp.sum(d_innorm * in_hat, axis=0),
            jnp.sum(d_innorm, axis=0),
            jnp.sum(d_outnorm * out_hat, axis=1),
            jnp.sum(d_outnorm, axis=1),
        ]
    )
    blocks = [dot(in_norm, part, 0, 1) for part in d_proj]
    blocks += [dot(in_norm, d_five, 0, 0), dot(out_norm, d_lin, 1, 0), norms]
    used, share, slots = 6 * c + 4, 200, 256
    stacked = jnp.concatenate(blocks + [jnp.zeros((4 * share - used, c), F32)])
    ours = jnp.sum(exchange(stacked.reshape(4, share, c), QUAD), axis=0)
    ours = jnp.pad(ours, ((0, slots - share), (0, 0))).reshape(32, slots // 32, c)
    mine = jnp.sum(exchange(ours, MID), axis=0)
    mine = mine + lax.ppermute(mine, "zq", [(0, 3), (3, 0), (1, 2), (2, 1)])
    mine = mine + lax.ppermute(mine, "zq", [(0, 1), (1, 0), (2, 3), (3, 2)])
    mine = jnp.broadcast_to((mine * (1.0 / all_k))[None], ours.shape)
    summed = exchange(mine, MID).reshape(slots, c)
    summed = lax.all_gather(summed[:share], QUAD).reshape(4 * share, c)
    grad_in = jnp.concatenate([summed[b * c : (b + 1) * c] for b in range(5)], axis=1)
    return (
        pair_out.reshape(ni, nk, c),
        grad_pair.reshape(ni, nk, c),
        grad_in,
        summed[5 * c : 6 * c],
        summed[6 * c : used],
    )


def solution(mesh):
    grid = mesh.devices.reshape(4, 4, 2, 2, 2, 2, 2)
    split = Mesh(grid, ("zq", "zr", "yl", "xh", "xl", "yh", "core"))
    pair = P(("zq", "zr", "yl"), ("xh", "xl", "yh", "core"), None)
    return jax.shard_map(
        local,
        mesh=split,
        in_specs=(pair, pair, P(), P(), P(), P(), P(), P()),
        out_specs=(pair, pair, P(), P(), P()),
        check_vma=False,
    )
```

```python
import jax
import jax.numpy as jnp
from jax import lax
from jax.sharding import Mesh, PartitionSpec as P

CUBE = ("zr", "yl", "xh", "xl", "yh", "core")
BF = jnp.bfloat16
F32 = jnp.float32


def dot(a, b, da, db):
    return lax.dot_general(a, b, (((da,), (db,)), ((), ())), preferred_element_type=F32)


def stats(values, axis):
    average = jnp.mean(values, axis=axis, keepdims=True)
    centred = values - average
    inv_std = lax.rsqrt(jnp.mean(centred * centred, axis=axis, keepdims=True) + 1e-05)
    return centred * inv_std, inv_std


def back(upstream, hat, inv_std, scaling, axis):
    scaled = upstream * scaling
    return inv_std * (
        scaled
        - jnp.mean(scaled, axis=axis, keepdims=True)
        - hat * jnp.mean(scaled * hat, axis=axis, keepdims=True)
    )


def exchange(x, axes=CUBE):
    return lax.all_to_all(x, axes, split_axis=0, concat_axis=0, tiled=True)


def local(pair_in, cotangent, in_gain, in_bias, in_weights, out_gain, out_bias, out_weights):
    ni, nk, c = pair_in.shape
    rr, cols, quarters = 8, 16, 4
    pairs = ni * nk
    rows, all_k = rr * ni, cols * nk

    def to_matrix(x):
        x = x.reshape(rr, cols, ni, nk).transpose(0, 2, 1, 3)
        return x.reshape(rows, all_k)

    def from_matrix(x):
        x = x.reshape(rr, ni, cols, nk).transpose(0, 2, 1, 3)
        return x.reshape(c, pairs)

    in_hat, in_rstd = stats(pair_in.reshape(pairs, c).astype(F32), 1)
    in_norm = (in_hat * in_gain + in_bias).astype(BF)
    w_gate = in_weights[:, 4 * c :]
    proj = dot(in_weights[:, : 4 * c], in_norm, 0, 1)
    gate = jax.nn.sigmoid(dot(in_norm, w_gate, 1, 0))
    lin_left, lin_right = proj[:c], proj[2 * c : 3 * c]
    left_sig = jax.nn.sigmoid(proj[c : 2 * c])
    right_sig = jax.nn.sigmoid(proj[3 * c :])
    left = (left_sig * lin_left).astype(BF)
    right = (right_sig * lin_right).astype(BF)

    got = exchange(jnp.concatenate([left, right], axis=1))
    left_own = to_matrix(got[:, :pairs])
    right_all = lax.all_gather(to_matrix(got[:, pairs:]), "zq").reshape(all_k, all_k)
    product = dot(left_own, right_all, 1, 1)
    prod = exchange(from_matrix(product))

    out_hat, out_rstd = stats(prod, 0)
    gain_col = out_gain[:, None]
    out_norm = (out_hat * gain_col + out_bias[:, None]).astype(BF)
    out_lin = dot(out_norm, out_weights, 0, 0)
    pair_out = (gate * out_lin).astype(BF)
    upstream = cotangent.reshape(pairs, c).astype(F32)
    d_lin = (upstream * gate).astype(BF)
    d_gate = upstream * out_lin
    d_outnorm = dot(out_weights, d_lin, 1, 1)
    d_product = back(d_outnorm, out_hat, out_rstd, gain_col, 0).astype(BF)

    d_mat = to_matrix(exchange(d_product))
    d_left_m = dot(d_mat, right_all, 1, 0).astype(BF)
    terms = dot(d_mat, left_own, 0, 0).astype(BF)
    terms = exchange(terms.reshape(quarters, rows, all_k), ("zq",))
    d_right_m = jnp.sum(terms.astype(F32), axis=0).astype(BF)
    d_both = exchange(jnp.concatenate([from_matrix(d_left_m), from_matrix(d_right_m)], axis=1))
    d_both = d_both.astype(F32)
    d_left, d_right = d_both[:, :pairs], d_both[:, pairs:]

    d_proj = [
        (d_left * left_sig).astype(BF),
        (d_left * lin_left * left_sig * (1.0 - left_sig)).astype(BF),
        (d_right * right_sig).astype(BF),
        (d_right * lin_right * right_sig * (1.0 - right_sig)).astype(BF),
    ]
    d_five = (d_gate * gate * (1.0 - gate)).astype(BF)
    d_innorm = dot(jnp.concatenate(d_proj), in_weights[:, : 4 * c], 0, 1) + dot(d_five, w_gate, 1, 1)
    grad_pair = back(d_innorm, in_hat, in_rstd, in_gain, 1).astype(BF)

    norms = jnp.stack(
        [
            jnp.sum(d_innorm * in_hat, axis=0),
            jnp.sum(d_innorm, axis=0),
            jnp.sum(d_outnorm * out_hat, axis=1),
            jnp.sum(d_outnorm, axis=1),
        ]
    )
    blocks = [dot(in_norm, part, 0, 1) for part in d_proj]
    blocks += [dot(in_norm, d_five, 0, 0), dot(out_norm, d_lin, 1, 0), norms]
    used, slots = 6 * c + 4, 8
    stacked = jnp.concatenate(blocks + [jnp.zeros((slots * c - used, c), F32)])
    mine = jnp.sum(exchange(stacked.reshape(c, slots, c)), axis=0)
    four = exchange(jnp.broadcast_to(mine[None], (quarters, slots, c)), ("zq",))
    mine = ((four[0] + four[1]) + (four[2] + four[3])) * (1.0 / all_k)
    summed = exchange(jnp.broadcast_to(mine.astype(BF)[None], (c, slots, c)))
    summed = summed.reshape(slots * c, c).astype(F32)
    grad_in = jnp.concatenate([summed[b * c : (b + 1) * c] for b in range(5)], axis=1)
    return (
        pair_out.reshape(ni, nk, c),
        grad_pair.reshape(ni, nk, c),
        grad_in,
        summed[5 * c : 6 * c],
        summed[6 * c : used],
    )


def solution(mesh):
    grid = mesh.devices.reshape(4, 4, 2, 2, 2, 2, 2)
    split = Mesh(grid, ("zq", "zr", "yl", "xh", "xl", "yh", "core"))
    pair = P(("zq", "zr", "yl"), ("xh", "xl", "yh", "core"), None)
    return jax.shard_map(
        local,
        mesh=split,
        in_specs=(pair, pair, P(), P(), P(), P(), P(), P()),
        out_specs=(pair, pair, P(), P(), P()),
        check_vma=False,
    )
```

```python
import jax
import jax.numpy as jnp
from jax import lax
from jax.sharding import Mesh, PartitionSpec as P

CUBE = ("zr", "yl", "xh", "xl", "yh", "core")
CHIPS = ("zr", "yl", "xh", "xl", "yh")
BF = jnp.bfloat16
F32 = jnp.float32


def dot(a, b, da, db):
    return lax.dot_general(a, b, (((da,), (db,)), ((), ())), preferred_element_type=F32)


def stats(values, axis):
    average = jnp.mean(values, axis=axis, keepdims=True)
    centred = values - average
    inv_std = lax.rsqrt(jnp.mean(centred * centred, axis=axis, keepdims=True) + 1e-05)
    return centred * inv_std, inv_std


def back(upstream, hat, inv_std, scaling, axis):
    scaled = upstream * scaling
    return inv_std * (
        scaled
        - jnp.mean(scaled, axis=axis, keepdims=True)
        - hat * jnp.mean(scaled * hat, axis=axis, keepdims=True)
    )


def exchange(x, axes=CUBE):
    return lax.all_to_all(x, axes, split_axis=0, concat_axis=0, tiled=True)


def local(pair_in, cotangent, in_gain, in_bias, in_weights, out_gain, out_bias, out_weights):
    ni, nk, c = pair_in.shape
    rr, cols, quarters = 8, 16, 4
    pairs = ni * nk
    rows, all_k = rr * ni, cols * nk

    def to_matrix(x):
        x = x.reshape(rr, cols, ni, nk).transpose(0, 2, 1, 3)
        return x.reshape(rows, all_k)

    def from_matrix(x):
        x = x.reshape(rr, ni, cols, nk).transpose(0, 2, 1, 3)
        return x.reshape(c, pairs)

    in_hat, in_rstd = stats(pair_in.reshape(pairs, c).astype(F32), 1)
    in_norm = (in_hat * in_gain + in_bias).astype(BF)
    w_gate = in_weights[:, 4 * c :]
    proj = dot(in_weights[:, : 4 * c], in_norm, 0, 1)
    gate = jax.nn.sigmoid(dot(in_norm, w_gate, 1, 0))
    lin_left, lin_right = proj[:c], proj[2 * c : 3 * c]
    left_sig = jax.nn.sigmoid(proj[c : 2 * c])
    right_sig = jax.nn.sigmoid(proj[3 * c :])
    left = (left_sig * lin_left).astype(BF)
    right = (right_sig * lin_right).astype(BF)

    got = exchange(jnp.concatenate([left, right], axis=1))
    left_own = to_matrix(got[:, :pairs])
    right_all = lax.all_gather(to_matrix(got[:, pairs:]), "zq").reshape(all_k, all_k)
    product = dot(left_own, right_all, 1, 1)
    prod = exchange(from_matrix(product))

    out_hat, out_rstd = stats(prod, 0)
    gain_col = out_gain[:, None]
    out_norm = (out_hat * gain_col + out_bias[:, None]).astype(BF)
    out_lin = dot(out_norm, out_weights, 0, 0)
    pair_out = (gate * out_lin).astype(BF)
    upstream = cotangent.reshape(pairs, c).astype(F32)
    d_lin = (upstream * gate).astype(BF)
    d_gate = upstream * out_lin
    d_outnorm = dot(out_weights, d_lin, 1, 1)
    d_product = back(d_outnorm, out_hat, out_rstd, gain_col, 0).astype(BF)

    d_mat = to_matrix(exchange(d_product))
    d_left_m = dot(d_mat, right_all, 1, 0).astype(BF)
    terms = dot(d_mat, left_own, 0, 0).astype(BF)
    terms = exchange(terms.reshape(quarters, rows, all_k), ("zq",))
    d_right_m = jnp.sum(terms.astype(F32), axis=0).astype(BF)
    d_both = exchange(jnp.concatenate([from_matrix(d_left_m), from_matrix(d_right_m)], axis=1))
    d_both = d_both.astype(F32)
    d_left, d_right = d_both[:, :pairs], d_both[:, pairs:]

    d_proj = [
        (d_left * left_sig).astype(BF),
        (d_left * lin_left * left_sig * (1.0 - left_sig)).astype(BF),
        (d_right * right_sig).astype(BF),
        (d_right * lin_right * right_sig * (1.0 - right_sig)).astype(BF),
    ]
    d_five = (d_gate * gate * (1.0 - gate)).astype(BF)
    d_innorm = dot(jnp.concatenate(d_proj), in_weights[:, : 4 * c], 0, 1) + dot(d_five, w_gate, 1, 1)
    grad_pair = back(d_innorm, in_hat, in_rstd, in_gain, 1).astype(BF)

    norms = jnp.stack(
        [
            jnp.sum(d_innorm * in_hat, axis=0),
            jnp.sum(d_innorm, axis=0),
            jnp.sum(d_outnorm * out_hat, axis=1),
            jnp.sum(d_outnorm, axis=1),
        ]
    )
    blocks = [dot(in_norm, part, 0, 1) for part in d_proj]
    blocks += [dot(in_norm, d_five, 0, 0), dot(out_norm, d_lin, 1, 0), norms]
    used, slots, peers = 6 * c + 4, 16, c // 2
    stacked = jnp.concatenate(blocks + [jnp.zeros((slots * peers - used, c), F32)]).astype(BF)
    mine = jnp.sum(exchange(stacked.reshape(peers, slots, c), CHIPS).astype(F32), axis=0)
    eight = exchange(jnp.broadcast_to(mine[None], (2 * quarters, slots, c)), ("zq", "core"))
    mine = (jnp.sum(eight, axis=0) * (1.0 / all_k)).astype(BF)
    summed = exchange(jnp.broadcast_to(mine[None], (peers, slots, c)), CHIPS)
    summed = summed.reshape(slots * peers, c).astype(F32)
    grad_in = jnp.concatenate([summed[b * c : (b + 1) * c] for b in range(5)], axis=1)
    return (
        pair_out.reshape(ni, nk, c),
        grad_pair.reshape(ni, nk, c),
        grad_in,
        summed[5 * c : 6 * c],
        summed[6 * c : used],
    )


def solution(mesh):
    grid = mesh.devices.reshape(4, 4, 2, 2, 2, 2, 2)
    split = Mesh(grid, ("zq", "zr", "yl", "xh", "xl", "yh", "core"))
    pair = P(("zq", "zr", "yl"), ("xh", "xl", "yh", "core"), None)
    return jax.shard_map(
        local,
        mesh=split,
        in_specs=(pair, pair, P(), P(), P(), P(), P(), P()),
        out_specs=(pair, pair, P(), P(), P()),
        check_vma=False,
    )
```

```python
import jax
import jax.numpy as jnp
from jax import lax
from jax.sharding import Mesh, PartitionSpec as P

CUBE = ("zr", "yl", "xh", "xl", "yh", "core")
CHIPS = ("zr", "yl", "xh", "xl", "yh")
BF = jnp.bfloat16
F32 = jnp.float32


def dot(a, b, da, db):
    return lax.dot_general(a, b, (((da,), (db,)), ((), ())), preferred_element_type=F32)


def stats(values, axis):
    average = jnp.mean(values, axis=axis, keepdims=True)
    centred = values - average
    inv_std = lax.rsqrt(jnp.mean(centred * centred, axis=axis, keepdims=True) + 1e-05)
    return centred * inv_std, inv_std


def back(upstream, hat, inv_std, scaling, axis):
    scaled = upstream * scaling
    return inv_std * (
        scaled
        - jnp.mean(scaled, axis=axis, keepdims=True)
        - hat * jnp.mean(scaled * hat, axis=axis, keepdims=True)
    )


def exchange(x, axes=CUBE):
    return lax.all_to_all(x, axes, split_axis=0, concat_axis=0, tiled=True)


def local(pair_in, cotangent, in_gain, in_bias, in_weights, out_gain, out_bias, out_weights):
    ni, nk, c = pair_in.shape
    rr, cols, quarters = 8, 16, 4
    pairs = ni * nk
    rows, all_k = rr * ni, cols * nk

    def to_matrix(x):
        x = x.reshape(rr, cols, 2, ni // 2, nk).transpose(0, 2, 3, 1, 4)
        return x.reshape(rows, all_k)

    def from_matrix(x):
        x = x.reshape(rr, ni, cols, nk).transpose(0, 2, 1, 3)
        return x.reshape(c, pairs)

    in_hat, in_rstd = stats(pair_in.reshape(pairs, c).astype(F32), 1)
    in_norm = (in_hat * in_gain + in_bias).astype(BF)
    w_gate = in_weights[:, 4 * c :]
    proj = dot(in_weights[:, : 4 * c], in_norm, 0, 1)
    gate = jax.nn.sigmoid(dot(in_norm, w_gate, 1, 0))
    lin_left, lin_right = proj[:c], proj[2 * c : 3 * c]
    left_sig = jax.nn.sigmoid(proj[c : 2 * c])
    right_sig = jax.nn.sigmoid(proj[3 * c :])
    left = (left_sig * lin_left).astype(BF)
    right = (right_sig * lin_right).astype(BF)

    got = exchange(jnp.stack([left, right], axis=1))
    left_own = to_matrix(got[:, 0])
    right_all = lax.all_gather(to_matrix(got[:, 1]), "zq").reshape(all_k, all_k)
    product = dot(left_own, right_all, 1, 1)
    prod = exchange(from_matrix(product))

    out_hat, out_rstd = stats(prod, 0)
    gain_col = out_gain[:, None]
    out_norm = (out_hat * gain_col + out_bias[:, None]).astype(BF)
    out_lin = dot(out_norm, out_weights, 0, 0)
    pair_out = (gate * out_lin).astype(BF)
    upstream = cotangent.reshape(pairs, c).astype(F32)
    d_lin = (upstream * gate).astype(BF)
    d_gate = upstream * out_lin
    d_outnorm = dot(out_weights, d_lin, 1, 1)
    d_product = back(d_outnorm, out_hat, out_rstd, gain_col, 0).astype(BF)

    d_mat = to_matrix(exchange(d_product.reshape(c, 2, pairs // 2)))
    d_left_m = dot(d_mat, right_all, 1, 0).astype(BF)
    terms = dot(d_mat, left_own, 0, 0).astype(BF)
    terms = exchange(terms.reshape(quarters, rows, all_k), ("zq",))
    d_right_m = jnp.sum(terms.astype(F32), axis=0).astype(BF)
    d_both = exchange(jnp.stack([from_matrix(d_left_m), from_matrix(d_right_m)], axis=1))
    d_both = d_both.astype(F32)
    d_left, d_right = d_both[:, 0], d_both[:, 1]

    d_proj = [
        (d_left * left_sig).astype(BF),
        (d_left * lin_left * left_sig * (1.0 - left_sig)).astype(BF),
        (d_right * right_sig).astype(BF),
        (d_right * lin_right * right_sig * (1.0 - right_sig)).astype(BF),
    ]
    d_five = (d_gate * gate * (1.0 - gate)).astype(BF)
    d_innorm = dot(jnp.concatenate(d_proj), in_weights[:, : 4 * c], 0, 1) + dot(d_five, w_gate, 1, 1)
    grad_pair = back(d_innorm, in_hat, in_rstd, in_gain, 1).astype(BF)

    norms = jnp.stack(
        [
            jnp.sum(d_innorm * in_hat, axis=0),
            jnp.sum(d_innorm, axis=0),
            jnp.sum(d_outnorm * out_hat, axis=1),
            jnp.sum(d_outnorm, axis=1),
        ]
    )
    blocks = [dot(in_norm, part, 0, 1) for part in d_proj]
    blocks += [dot(in_norm, d_five, 0, 0), dot(out_norm, d_lin, 1, 0), norms]
    used, slots, peers = 6 * c + 4, 16, c // 2
    stacked = jnp.concatenate(blocks + [jnp.zeros((slots * peers - used, c), F32)]).astype(BF)
    mine = jnp.sum(exchange(stacked.reshape(peers, slots, c), CHIPS).astype(F32), axis=0)
    eight = exchange(jnp.broadcast_to(mine[None], (2 * quarters, slots, c)), ("zq", "core"))
    mine = (jnp.sum(eight, axis=0) * (1.0 / all_k)).astype(BF)
    summed = exchange(jnp.broadcast_to(mine[None], (peers, slots, c)), CHIPS)
    summed = summed.reshape(slots * peers, c).astype(F32)
    grad_in = jnp.concatenate([summed[b * c : (b + 1) * c] for b in range(5)], axis=1)
    return (
        pair_out.reshape(ni, nk, c),
        grad_pair.reshape(ni, nk, c),
        grad_in,
        summed[5 * c : 6 * c],
        summed[6 * c : used],
    )


def solution(mesh):
    grid = mesh.devices.reshape(4, 4, 2, 2, 2, 2, 2)
    split = Mesh(grid, ("zq", "zr", "yl", "xh", "xl", "yh", "core"))
    pair = P(("zq", "zr", "yl"), ("xh", "xl", "yh", "core"), None)
    return jax.shard_map(
        local,
        mesh=split,
        in_specs=(pair, pair, P(), P(), P(), P(), P(), P()),
        out_specs=(pair, pair, P(), P(), P()),
        check_vma=False,
    )
```

```python
import jax
import jax.numpy as jnp
from jax import lax
from jax.sharding import Mesh, PartitionSpec as P

CUBE = ("zr", "yl", "xh", "xl", "yh", "core")
CHIPS = ("zr", "yl", "xh", "xl", "yh")
BF = jnp.bfloat16
F32 = jnp.float32


def dot(a, b, da, db):
    return lax.dot_general(a, b, (((da,), (db,)), ((), ())), preferred_element_type=F32)


def stats(values, axis):
    average = jnp.mean(values, axis=axis, keepdims=True)
    centred = values - average
    inv_std = lax.rsqrt(jnp.mean(centred * centred, axis=axis, keepdims=True) + 1e-05)
    return centred * inv_std, inv_std


def back(upstream, hat, inv_std, scaling, axis):
    scaled = upstream * scaling
    return inv_std * (
        scaled
        - jnp.mean(scaled, axis=axis, keepdims=True)
        - hat * jnp.mean(scaled * hat, axis=axis, keepdims=True)
    )


def exchange(x, axes=CUBE):
    return lax.all_to_all(x, axes, split_axis=0, concat_axis=0, tiled=True)


def local(pair_in, cotangent, in_gain, in_bias, in_weights, out_gain, out_bias, out_weights):
    ni, nk, c = pair_in.shape
    rr, cols, quarters = 8, 16, 4
    pairs = ni * nk
    rows, all_k = rr * ni, cols * nk

    def to_matrix(x):
        x = x.reshape(rr, cols, 2, ni // 2, nk).transpose(0, 2, 3, 1, 4)
        return x.reshape(rows, all_k)

    def from_matrix(x):
        x = x.reshape(rr, ni, cols, nk).transpose(0, 2, 1, 3)
        return x.reshape(c, pairs)

    in_hat, in_rstd = stats(pair_in.reshape(pairs, c).astype(F32), 1)
    in_norm = (in_hat * in_gain + in_bias).astype(BF)
    w_gate = in_weights[:, 4 * c :]
    proj = dot(in_weights[:, : 4 * c], in_norm, 0, 1)
    gate = jax.nn.sigmoid(dot(in_norm, w_gate, 1, 0))
    lin_left, lin_right = proj[:c], proj[2 * c : 3 * c]
    left_sig = jax.nn.sigmoid(proj[c : 2 * c])
    right_sig = jax.nn.sigmoid(proj[3 * c :])
    left = (left_sig * lin_left).astype(BF)
    right = (right_sig * lin_right).astype(BF)

    got = exchange(jnp.stack([left, right], axis=1))
    left_own = to_matrix(got[:, 0])
    right_all = lax.all_gather(to_matrix(got[:, 1]), "zq").reshape(all_k, all_k)
    product = dot(left_own, right_all, 1, 1)
    upstream = cotangent.reshape(pairs, c).astype(F32)
    d_lin = (upstream * gate).astype(BF)
    d_outnorm = dot(out_weights, d_lin, 1, 1)
    product, d_outnorm = lax.optimization_barrier((product, d_outnorm))
    prod = exchange(from_matrix(product))

    out_hat, out_rstd = stats(prod, 0)
    gain_col = out_gain[:, None]
    out_norm = (out_hat * gain_col + out_bias[:, None]).astype(BF)
    out_lin = dot(out_norm, out_weights, 0, 0)
    pair_out = (gate * out_lin).astype(BF)
    d_gate = upstream * out_lin
    d_product = back(d_outnorm, out_hat, out_rstd, gain_col, 0).astype(BF)

    d_mat = to_matrix(exchange(d_product.reshape(c, 2, pairs // 2)))
    d_left_m = dot(d_mat, right_all, 1, 0).astype(BF)
    terms = dot(d_mat, left_own, 0, 0).astype(BF)
    terms = exchange(terms.reshape(quarters, rows, all_k), ("zq",))
    d_right_m = jnp.sum(terms.astype(F32), axis=0).astype(BF)
    d_both = exchange(jnp.stack([from_matrix(d_left_m), from_matrix(d_right_m)], axis=1))
    d_both = d_both.astype(F32)
    d_left, d_right = d_both[:, 0], d_both[:, 1]

    d_proj = [
        (d_left * left_sig).astype(BF),
        (d_left * lin_left * left_sig * (1.0 - left_sig)).astype(BF),
        (d_right * right_sig).astype(BF),
        (d_right * lin_right * right_sig * (1.0 - right_sig)).astype(BF),
    ]
    d_five = (d_gate * gate * (1.0 - gate)).astype(BF)
    d_innorm = dot(jnp.concatenate(d_proj), in_weights[:, : 4 * c], 0, 1) + dot(d_five, w_gate, 1, 1)
    grad_pair = back(d_innorm, in_hat, in_rstd, in_gain, 1).astype(BF)

    norms = jnp.stack(
        [
            jnp.sum(d_innorm * in_hat, axis=0),
            jnp.sum(d_innorm, axis=0),
            jnp.sum(d_outnorm * out_hat, axis=1),
            jnp.sum(d_outnorm, axis=1),
        ]
    )
    blocks = [dot(in_norm, part, 0, 1) for part in d_proj]
    blocks += [dot(in_norm, d_five, 0, 0), dot(out_norm, d_lin, 1, 0), norms]
    used, slots, peers = 6 * c + 4, 16, c // 2
    stacked = jnp.concatenate(blocks + [jnp.zeros((slots * peers - used, c), F32)]).astype(BF)
    mine = jnp.sum(exchange(stacked.reshape(peers, slots, c), CHIPS).astype(F32), axis=0)
    eight = exchange(jnp.broadcast_to(mine[None], (2 * quarters, slots, c)), ("zq", "core"))
    mine = (jnp.sum(eight, axis=0) * (1.0 / all_k)).astype(BF)
    summed = exchange(jnp.broadcast_to(mine[None], (peers, slots, c)), CHIPS)
    summed = summed.reshape(slots * peers, c).astype(F32)
    grad_in = jnp.concatenate([summed[b * c : (b + 1) * c] for b in range(5)], axis=1)
    return (
        pair_out.reshape(ni, nk, c),
        grad_pair.reshape(ni, nk, c),
        grad_in,
        summed[5 * c : 6 * c],
        summed[6 * c : used],
    )


def solution(mesh):
    grid = mesh.devices.reshape(4, 4, 2, 2, 2, 2, 2)
    split = Mesh(grid, ("zq", "zr", "yl", "xh", "xl", "yh", "core"))
    pair = P(("zq", "zr", "yl"), ("xh", "xl", "yh", "core"), None)
    return jax.shard_map(
        local,
        mesh=split,
        in_specs=(pair, pair, P(), P(), P(), P(), P(), P()),
        out_specs=(pair, pair, P(), P(), P()),
        check_vma=False,
    )
```
